32 devices in a mesh: dp: 8 (over z, core), feat: 4 (over y, x).
Axes of the slice: x: 2, y: 2, z: 4, core: 2. Of those that a mesh axis runs over, the one named last changes fastest.
Arguments:
- points: bfloat16 [2048, 256], P('dp'), may hold values from -6 to 6
- freqs: bfloat16 [256, 8192], P(None, 'feat'), may hold values from -0.375 to 0.375
- phase: float32 [8192], P('feat'), may hold values from -3.140625 to 3.140625
- ridge: float32 [8192], P('feat'), may hold values from 0.05 to 0.5
- targets: bfloat16 [8, 2048], P(None, 'dp'), may hold values from -6 to 6
Outputs:
- gram: float32 [8192, 8192], P('feat', 'dp')
- projected: float32 [8, 8192], P(None, 'feat')
- factors: float32 [8192, 1024], P('feat')
The draws below stay inside these ranges and needn't reach their ends.
All inputs are finite; a program needn't handle non-finite values.
Results may differ from the reference program's by a relative error of at most 0.003.
Values may be sent and summed in bfloat16 or wider, within the bound.
A program may use at most 128 MiB of HBM per device.

```python
import math
import jax
import jax.numpy as jnp
from jax import lax

DIN = 256
OUTS = 8
FB = 1024
F = 8192
ROWS = 2048


def steps_of(rng, shape, pieces, smallest, top_value):
    def one(position, blocks):
        steps = jax.random.uniform(jax.random.fold_in(jax.random.fold_in(rng, 6), position), (blocks,), jnp.float32, smallest / len(pieces), top_value / len(pieces))
        return jnp.repeat(jnp.exp(steps), shape[position] // blocks).reshape((-1,) + (1,) * (len(shape) - position - 1))

    gain = one(*pieces[0])
    for cut in pieces[1:]:
        gain = gain * one(*cut)
    return gain


def gaussian(own_key, extent, spread, limit, cuts=(), held_as=jnp.bfloat16):
    array = jax.random.normal(own_key, extent, jnp.float32) * spread
    if len(cuts) > 0:
        array = steps_of(own_key, extent, cuts, -0.22, 0.18) * array
    return jnp.clip(array, min=-limit, max=limit).astype(held_as)


def setup_inputs(seed: int = 0) -> dict:
    keys = jax.random.split(jax.random.key(seed), 6)
    points = gaussian(keys[0], (ROWS, DIN), 1.0, 6.0, ((0, 8),))
    freqs = gaussian(keys[1], (DIN, F), DIN ** -0.5, 0.375, ((1, 4),))
    phase = jnp.clip(jax.random.uniform(keys[2], (F,), jnp.float32, -3.140625, 3.140625), -3.140625, 3.140625)
    ridge = jnp.clip(jnp.exp(math.log(0.5) - 2.3025851 * jax.random.uniform(keys[3], (F,), jnp.float32) ** steps_of(keys[3], (F,), ((0, 4),), -0.2, 0.2)), 0.05, 0.5)
    targets = gaussian(keys[4], (OUTS, ROWS), 1.0, 6.0, ((1, 8),))
    return {"points": points, "freqs": freqs, "phase": phase, "ridge": ridge, "targets": targets}


def reference(points, freqs, phase, ridge, targets):
    scale = math.sqrt(2.0 / ROWS)
    angle = jnp.dot(points.astype(jnp.float32), freqs.astype(jnp.float32), preferred_element_type=jnp.float32) + phase
    phi = (scale * jnp.cos(angle)).astype(jnp.bfloat16)
    phi_wide = phi.astype(jnp.float32)
    gram = jnp.dot(phi_wide.T, phi_wide, precision=lax.Precision.HIGHEST) + jnp.diag(ridge)
    projected = jnp.dot(targets.astype(jnp.float32), phi_wide, precision=lax.Precision.HIGHEST)
    blocks = jnp.stack([gram[block_number * FB:(block_number + 1) * FB, block_number * FB:(block_number + 1) * FB] for block_number in range(OUTS)])
    factors = jnp.linalg.cholesky(blocks).reshape(F, FB)
    return (gram, projected, factors)
```

```python
import functools
import math

import jax
import jax.numpy as jnp
from jax import lax
from jax.experimental import pallas as pl
from jax.experimental.pallas import tpu as pltpu
from jax.sharding import PartitionSpec as P

FB = 1024
TILE = 128
MICRO = 16
SIN_TURNS = (3.1415925797889983, -5.167706865106645, 2.550031175689404, -0.5980440852345476, 0.07721816880214098)


def features(rows, freq_cols, phase_cols, scale):
    angle = jnp.dot(rows, freq_cols, preferred_element_type=jnp.float32) + phase_cols
    turns = angle * (0.5 / math.pi)
    part = turns - jnp.round(turns)
    square = part * part
    poly = jnp.full_like(square, SIN_TURNS[-1])
    for coeff in SIN_TURNS[-2::-1]:
        poly = poly * square + coeff
    sine = poly * part
    return (scale - (2.0 * scale) * (sine * sine)).astype(jnp.bfloat16)


def cross(left, right):
    return lax.dot_general(
        left, right, (((0,), (0,)), ((), ())), preferred_element_type=jnp.float32
    )


def with_ridge(tile, ridge, row_start, col_start):
    rows_here = row_start + lax.broadcasted_iota(jnp.int32, tile.shape, 0)
    cols_here = col_start + lax.broadcasted_iota(jnp.int32, tile.shape, 1)
    return tile + jnp.where(rows_here == cols_here, ridge[:, None], 0.0)


def halves(value):
    high = value.astype(jnp.bfloat16)
    return high, (value - high.astype(jnp.float32)).astype(jnp.bfloat16)


def left_parts(value, axis):
    high, low = halves(value)
    return jnp.concatenate([high, high, low], axis=axis)


def right_parts(value):
    high, low = halves(value)
    return jnp.concatenate([high, low, high], axis=0)


def panel_rows(rows_lead, rows_tail, start):
    shape = rows_lead.shape
    row_ids = lax.broadcasted_iota(jnp.int32, shape, 0)
    cols = [
        jnp.broadcast_to(rows_lead[:, start + i : start + i + 1], shape) for i in range(MICRO)
    ]
    for i in range(MICRO):
        inv = lax.rsqrt(cols[i][i : i + 1, :])
        mult = cols[i] * inv
        for m in range(i + 1, MICRO):
            cols[m] = cols[m] - mult * mult[m : m + 1, :]
        below = jnp.where(row_ids > i, mult, 0.0)
        here = row_ids == i
        lead = rows_lead[i : i + 1, :] * inv
        tail = rows_tail[i : i + 1, :] * inv
        rows_lead = jnp.where(here, lead, rows_lead - below * lead)
        rows_tail = jnp.where(here, tail, rows_tail - below * tail)
    return rows_lead, rows_tail


def chol_body(source, out, work, panel, sem, *, count, size):
    tiles = size // TILE
    copy = pltpu.make_async_copy(source, work, sem)
    copy.start()
    copy.wait()
    row_ids = lax.broadcasted_iota(jnp.int32, (TILE, TILE), 0)
    col_ids = lax.broadcasted_iota(jnp.int32, (TILE, TILE), 1)

    def step(k, carry):
        at = pl.multiple_of(k * TILE, TILE)
        for blk in range(count):
            panel[blk, :, :TILE] = work[blk, pl.ds(at, TILE), pl.ds(at, TILE)]
            panel[blk, :, TILE:] = jnp.where(row_ids == col_ids, 1.0, 0.0)
        for start in range(0, TILE, MICRO):
            end = start + MICRO
            for blk in range(count):
                lead, tail = panel_rows(
                    panel[blk, start:end, :TILE], panel[blk, start:end, TILE:], start
                )
                panel[blk, start:end, :TILE] = lead
                panel[blk, start:end, TILE:] = tail
                if end < TILE:
                    left = left_parts(lead, 0)
                    right = right_parts(jnp.concatenate([lead, tail], axis=1))
                    panel[blk, end:, :] = panel[blk, end:, :] - cross(left, right)[end:, :]
        for blk in range(count):
            lower = jnp.where(row_ids >= col_ids, panel[blk, :, :TILE].T, 0.0)
            out[blk, pl.ds(at, TILE), pl.ds(at, TILE)] = lower
        for c in range(tiles - 1):

            @pl.when(k == c)
            def _():
                lo, mid = c * TILE, (c + 1) * TILE
                for blk in range(count):
                    upper = jnp.dot(
                        left_parts(panel[blk, :, TILE:], 1),
                        right_parts(work[blk, lo:mid, mid:]),
                        preferred_element_type=jnp.float32,
                    )
                    lower = upper.T
                    out[blk, mid:, lo:mid] = lower
                    out[blk, lo:mid, mid:] = jnp.zeros_like(upper)
                    left = left_parts(lower, 1)
                    right = right_parts(upper)
                    rest = size - mid
                    for first in range(0, rest, 2 * TILE):
                        last = min(first + 2 * TILE, rest)
                        update = jnp.dot(
                            left[first:last], right[:, first:], preferred_element_type=jnp.float32
                        )
                        r = mid + first
                        work[blk, r : mid + last, r:] = work[blk, r : mid + last, r:] - update

        return carry

    lax.fori_loop(0, tiles, step, 0)


def lower_factors(blocks):
    count, size, _ = blocks.shape
    return pl.pallas_call(
        functools.partial(chol_body, count=count, size=size),
        out_shape=jax.ShapeDtypeStruct(blocks.shape, jnp.float32),
        in_specs=[pl.BlockSpec(memory_space=pl.ANY)],
        out_specs=pl.BlockSpec(memory_space=pltpu.VMEM),
        scratch_shapes=[
            pltpu.VMEM(blocks.shape, jnp.float32),
            pltpu.VMEM((count, TILE, 2 * TILE), jnp.float32),
            pltpu.SemaphoreType.DMA,
        ],
        compiler_params=pltpu.CompilerParams(vmem_limit_bytes=48 * 1024 * 1024),
        name="lower_factors",
    )(blocks)


def shards(points, freqs, phase, ridge, targets):
    data_count = lax.axis_size("dp")
    feat_count = lax.axis_size("feat")
    feat_index = lax.axis_index("feat")
    data_index = lax.axis_index("dp")
    local_width = freqs.shape[1]
    total_width = local_width * feat_count
    tile_width = total_width // data_count
    window = max(local_width, FB)
    window_start = feat_index * local_width // window * window
    row_start = feat_index * local_width
    col_start = data_index * tile_width
    scale = math.sqrt(2.0 / (points.shape[0] * data_count))
    points_all = lax.all_gather(points, "dp", axis=0, tiled=True)
    targets_all = lax.all_gather(targets, "dp", axis=1, tiled=True)
    freqs_all = lax.all_gather(freqs, "feat", axis=1, tiled=True)
    phase_all, ridge_all = lax.all_gather(jnp.stack([phase, ridge]), "feat", axis=1, tiled=True)
    if window == local_width:
        window_phi = features(points_all, freqs, phase, scale)
        row_phi = window_phi
        window_ridge = ridge
    else:
        window_phi = features(
            points_all,
            lax.dynamic_slice_in_dim(freqs_all, window_start, window, 1),
            lax.dynamic_slice_in_dim(phase_all, window_start, window, 0),
            scale,
        )
        row_phi = lax.dynamic_slice_in_dim(
            window_phi, row_start - window_start, local_width, 1
        )
        window_ridge = lax.dynamic_slice_in_dim(ridge_all, window_start, window, 0)
    blocks = []
    for first in range(0, window, FB):
        part = window_phi[:, first : first + FB]
        blocks.append(with_ridge(cross(part, part), window_ridge[first : first + FB], 0, 0))
    factors_all = lower_factors(jnp.stack(blocks)).reshape(window, FB)
    factor_rows = lax.dynamic_slice_in_dim(factors_all, row_start - window_start, local_width, 0)
    col_phi = features(
        points_all,
        lax.dynamic_slice_in_dim(freqs_all, col_start, tile_width, 1),
        lax.dynamic_slice_in_dim(phase_all, col_start, tile_width, 0),
        scale,
    )
    gram_tile = with_ridge(cross(row_phi, col_phi), ridge, row_start, col_start)
    projected = jnp.dot(targets_all, row_phi, preferred_element_type=jnp.float32)
    return (gram_tile, projected, factor_rows)


def solution(mesh):
    in_specs = (P("dp", None), P(None, "feat"), P("feat"), P("feat"), P(None, "dp"))
    out_specs = (P("feat", "dp"), P(None, "feat"), P("feat", None))
    return jax.shard_map(shards, mesh=mesh, in_specs=in_specs, out_specs=out_specs, check_vma=False)
```
